32 devices in a mesh: grp: 4 (over y, core), leaf: 8 (over z, x).
Axes of the slice: x: 2, y: 2, z: 4, core: 2. Of those that a mesh axis runs over, the one named last changes fastest.
Arguments:
- points: bfloat16 [131072, 64], P(('grp', 'leaf')), may hold values from -6 to 6
- solution: float32 [131072, 64], P(('grp', 'leaf')), may hold values from -6 to 6
- residual: float32 [131072, 64], P(('grp', 'leaf')), may hold values from -150 to 150
- direction: float32 [131072, 64], P(('grp', 'leaf')), may hold values from -150 to 150
- near: int32 [128, 3], P(('grp', 'leaf')), may hold values from -1 to 127, as said below
- bases: bfloat16 [128, 1024, 256], P(('grp', 'leaf')), may hold values from -0.1875 to 0.1875
- leaf_transfer: bfloat16 [128, 256, 256], P(('grp', 'leaf')), may hold values from -0.1875 to 0.1875
- inner_transfer: bfloat16 [3, 2, 256, 256], replicated, may hold values from -1 to 1
- inner_coupling: bfloat16 [3, 256, 256], replicated, may hold values from -1 to 1
- outer_transfer: bfloat16 [2, 2, 256, 256], replicated, may hold values from -1 to 1
- outer_coupling: bfloat16 [2, 256, 256], replicated, may hold values from -1 to 1
Outputs:
- new_solution: float32 [131072, 64], P(('grp', 'leaf'))
- new_residual: float32 [131072, 64], P(('grp', 'leaf'))
- new_direction: float32 [131072, 64], P(('grp', 'leaf'))
The draws below stay inside these ranges and needn't reach their ends.
Inputs may be any that keep to these rules, and one draw needn't show every extreme that they name: Row i of near is (i, i - 1 or -1, i + 1 or -1); leaf i lists i + 1 exactly when leaf i + 1 lists i; the last leaf of each aligned block of 4 leaves lists the next leaf whenever there is one.
All inputs are finite; a program needn't handle non-finite values.
Results may differ from the reference program's by a relative error of at most 0.0027.
Values may be sent and summed in bfloat16 or wider, within the bound.
A program may use at most 128 MiB of HBM per device.

```python
import jax
import jax.numpy as jnp
from jax import lax

DIM = 64
LEAF = 1024
RANK = 256
NRHS = 64
LEAF_DEV = 4
LEAVES = 128
POINTS = 131072
LEVELS_LEAF = 3
LEVELS_GRP = 2
DEVICES = 32


def scaled_rows(key):
    first, second, third = jax.random.split(key, 3)
    where_row = jnp.arange(POINTS, dtype=jnp.float32) / POINTS
    col_scale = jnp.exp(jax.random.uniform(third, (NRHS,), jnp.float32) * jnp.log(10.0)) / jnp.sqrt(10.0)
    row_spread = jnp.exp(jax.random.uniform(second, (POINTS,), jnp.float32) * jnp.log(10.0))
    base = jnp.clip(jax.random.normal(first, (POINTS, NRHS), jnp.float32), -6.0, 6.0)
    row_scale = (1.0 + 2.0 * where_row) * row_spread / 4.0
    return base * row_scale[:, None] * col_scale[None, :]


def draw_residual(key, part):
    return scaled_rows(jax.random.fold_in(key, 101))


def draw_direction(key, part):
    return scaled_rows(jax.random.fold_in(key, 202))


def draw_near(key, part):
    links = jax.random.randint(jax.random.fold_in(key, 303), (LEAVES - 1,), 0, 4) > 0
    index = jnp.arange(LEAVES, dtype=jnp.int32)
    forced = (index[:-1] + 1) % LEAF_DEV == 0
    links = jnp.logical_or(links, forced)
    has_left = jnp.concatenate([jnp.zeros((1,), bool), links])
    has_right = jnp.concatenate([links, jnp.zeros((1,), bool)])
    left = jnp.where(has_left, index - 1, -1)
    right = jnp.where(has_right, index + 1, -1)
    return jnp.stack([index, left, right], axis=1).astype(jnp.int32)


def signed_table(key, shape, spread, clip_at):
    return jnp.clip(jax.random.normal(key, shape, jnp.float32), -clip_at, clip_at) * spread


def transfer_spread():
    return (70.0 / (99.0 * RANK)) ** 0.5


def coupling_spread():
    return 0.5 / RANK ** 0.5


def draw_bases(key, part):
    return signed_table(jax.random.fold_in(key, 808), (LEAVES, LEAF, RANK), LEAF ** (-0.5), 6.0).astype(jnp.bfloat16)


def draw_leaf_transfer(key, part):
    return signed_table(jax.random.fold_in(key, 909), (LEAVES, RANK, RANK), (LEAF_DEV * RANK) ** (-0.5), 6.0).astype(jnp.bfloat16)


def draw_inner_transfer(key, part):
    return signed_table(jax.random.fold_in(key, 404), (LEVELS_LEAF, 2, RANK, RANK), transfer_spread(), 4.0).astype(jnp.bfloat16)


def draw_outer_transfer(key, part):
    return signed_table(jax.random.fold_in(key, 505), (LEVELS_GRP, 2, RANK, RANK), transfer_spread(), 4.0).astype(jnp.bfloat16)


def draw_inner_coupling(key, part):
    return signed_table(jax.random.fold_in(key, 606), (LEVELS_LEAF, RANK, RANK), coupling_spread(), 4.0).astype(jnp.bfloat16)


def draw_outer_coupling(key, part):
    return signed_table(jax.random.fold_in(key, 707), (LEVELS_GRP, RANK, RANK), coupling_spread(), 4.0).astype(jnp.bfloat16)


def block_levels(rng, extent, cuts, low, top_value):
    def one(position, parts):
        draws = jax.random.uniform(jax.random.fold_in(jax.random.fold_in(rng, 6), position), (parts,), jnp.float32, low / len(cuts), top_value / len(cuts))
        return jnp.repeat(jnp.exp(draws), extent[position] // parts).reshape((-1,) + (1,) * (len(extent) - position - 1))

    loudness = one(*cuts[0])
    for cut in cuts[1:]:
        loudness = loudness * one(*cut)
    return loudness


def noise(key, extent, scale, reach, cuts=(), kind=jnp.bfloat16):
    drawn = scale * jax.random.normal(key, extent, jnp.float32)
    if cuts:
        drawn = drawn * block_levels(key, extent, cuts, -0.22, 0.18)
    return jnp.clip(drawn, -reach, reach).astype(kind)


def setup_inputs(seed: int = 0) -> dict:
    streams_of = jax.random.split(jax.random.key(seed), 12)
    return {
        "points": noise(streams_of[0], (POINTS, DIM), 1.0, 6.0, ((0, 32),)),
        "solution": noise(streams_of[1], (POINTS, NRHS), 1.0, 6.0, ((0, 32),), jnp.float32),
        "residual": draw_residual(jax.random.fold_in(streams_of[11], 71), 0),
        "direction": draw_direction(jax.random.fold_in(streams_of[11], 71), 0),
        "near": draw_near(jax.random.fold_in(streams_of[11], 71), 0),
        "bases": draw_bases(jax.random.fold_in(streams_of[11], 71), 0),
        "leaf_transfer": draw_leaf_transfer(jax.random.fold_in(streams_of[11], 71), 0),
        "inner_transfer": draw_inner_transfer(jax.random.fold_in(streams_of[11], 71), 0),
        "inner_coupling": draw_inner_coupling(jax.random.fold_in(streams_of[11], 71), 0),
        "outer_transfer": draw_outer_transfer(jax.random.fold_in(streams_of[11], 71), 0),
        "outer_coupling": draw_outer_coupling(jax.random.fold_in(streams_of[11], 71), 0),
    }


highest = lax.Precision.HIGHEST
ridge = 2.0


def kernel_block(own, window, mask):
    own_wide = own.astype(jnp.float32)
    win_wide = window.astype(jnp.float32)
    sq_own = jnp.sum(own_wide * own_wide, axis=1)
    sq_win = jnp.sum(win_wide * win_wide, axis=1)
    cross = jnp.dot(own, window.T, preferred_element_type=jnp.float32)
    dist = sq_own[:, None] + sq_win[None, :] - 2.0 * cross
    return (jnp.exp(-dist * (2.0 / own.shape[1])) * mask[None, :]).astype(jnp.bfloat16)


def near_field(points, packed, near):
    def one(index):
        ids = near[index]
        order = [ids[1], ids[0], ids[2]]
        pts_list = []
        vec_list = []
        mask_list = []
        for ident in order:
            start = (jnp.clip(ident, 0, LEAVES - 1) * LEAF).astype(jnp.int32)
            pts_list.append(lax.dynamic_slice_in_dim(points, start, LEAF, 0))
            vec_list.append(lax.dynamic_slice_in_dim(packed, start, LEAF, 0))
            mask_list.append(jnp.where(ident >= 0, 1.0, 0.0).astype(jnp.float32) * jnp.ones((LEAF,), jnp.float32))
        own = lax.dynamic_slice_in_dim(points, (index * LEAF).astype(jnp.int32), LEAF, 0)
        kern = kernel_block(own, jnp.concatenate(pts_list, 0), jnp.concatenate(mask_list, 0))
        return jnp.dot(kern, jnp.concatenate(vec_list, 0), preferred_element_type=jnp.float32)

    result = lax.map(one, jnp.arange(LEAVES, dtype=jnp.int32))
    return result.reshape(POINTS, NRHS)


def far_field(packed, bases, leaf_transfer, inner_transfer, inner_coupling, outer_transfer, outer_coupling):
    vectors = packed.reshape(LEAVES, LEAF, NRHS).astype(jnp.float32)
    skel = jnp.einsum('lpr,lpc->lrc', bases.astype(jnp.float32), vectors, precision=highest)
    trans = leaf_transfer.astype(jnp.float32).reshape(DEVICES, LEAF_DEV, RANK, RANK)
    nodes = jnp.einsum('dlba,dlbc->dac', trans, skel.reshape(DEVICES, LEAF_DEV, RANK, NRHS), precision=highest)
    q_all = jnp.concatenate([inner_transfer, outer_transfer], 0).astype(jnp.float32)
    b_all = jnp.concatenate([inner_coupling, outer_coupling], 0).astype(jnp.float32)
    couplings = []
    for level in range(q_all.shape[0]):
        left = nodes[0::2]
        right = nodes[1::2]
        to_left = jnp.einsum('ab,nbc->nac', b_all[level], right, precision=highest)
        to_right = jnp.einsum('ba,nbc->nac', b_all[level], left, precision=highest)
        couplings.append((to_left, to_right))
        nodes = jnp.einsum('ba,nbc->nac', q_all[level, 0], left, precision=highest) + jnp.einsum('ba,nbc->nac', q_all[level, 1], right, precision=highest)
    incoming = jnp.zeros((1, RANK, NRHS), jnp.float32)
    for level in reversed(range(q_all.shape[0])):
        to_left, to_right = couplings[level]
        left_in = to_left + jnp.einsum('ab,nbc->nac', q_all[level, 0], incoming, precision=highest)
        right_in = to_right + jnp.einsum('ab,nbc->nac', q_all[level, 1], incoming, precision=highest)
        incoming = jnp.stack([left_in, right_in], 1).reshape(-1, RANK, NRHS)
    leaf_in = jnp.einsum('dlab,dbc->dlac', trans, incoming, precision=highest).reshape(LEAVES, RANK, NRHS).astype(jnp.bfloat16)
    result = jnp.einsum('lpr,lrc->lpc', bases.astype(jnp.float32), leaf_in.astype(jnp.float32), precision=highest)
    return result.reshape(POINTS, NRHS)


def reference(points, solution, residual, direction, near, bases, leaf_transfer, inner_transfer, inner_coupling, outer_transfer, outer_coupling):
    packed = direction.astype(jnp.bfloat16)
    near_term = near_field(points, packed, near)
    far_term = far_field(packed, bases, leaf_transfer, inner_transfer, inner_coupling, outer_transfer, outer_coupling)
    image = ridge * direction + near_term + far_term
    rr = jnp.sum(residual * residual, axis=0)
    pq = jnp.sum(direction * image, axis=0)
    alpha = rr / pq
    new_solution = solution + alpha * direction
    new_residual = residual - alpha * image
    fresh = jnp.sum(new_residual * new_residual, axis=0)
    new_direction = new_residual + (fresh / rr) * direction
    return new_solution, new_residual, new_direction
```

```python
import functools
import math

import jax
import jax.numpy as jnp
from jax import lax
from jax.experimental import pallas as pl
from jax.experimental.pallas import tpu as pltpu
from jax.sharding import PartitionSpec as P

MESH = pl.DeviceIdType.MESH
ridge = 2.0
f32 = jnp.float32
bf16 = jnp.bfloat16
vmem = pl.BlockSpec(memory_space=pltpu.VMEM)
smem = pl.BlockSpec(memory_space=pltpu.SMEM)


def nn(a, b):
    return jnp.dot(a, b, preferred_element_type=f32)


def nt(a, b):
    return lax.dot_general(a, b, (((1,), (1,)), ((), ())), preferred_element_type=f32)


def split(value):
    high = value.astype(bf16)
    low = (value - high.astype(f32)).astype(bf16)
    return jnp.concatenate([high, low], axis=0)


def fold(stacked):
    half = stacked.shape[0] // 2
    return stacked[:half] + stacked[half:]


def upward_kernel(points_ref, direction_ref, bases_ref, trans_ref, joint_ref, node_ref, acc):
    step = pl.program_id(0)
    dim = points_ref.shape[0]
    packed = direction_ref[...].astype(bf16)
    joint_ref[:dim, :] = points_ref[...]
    joint_ref[dim:, :] = packed
    term = fold(nn(split(nn(packed, bases_ref[0])), trans_ref[0]))

    @pl.when(step == 0)
    def _():
        acc[...] = term

    @pl.when(step > 0)
    def _():
        acc[...] += term

    @pl.when(step == pl.num_programs(0) - 1)
    def _():
        node_ref[...] = split(acc[...])


def tree_kernel(
    groups, leaves, leaf, node_ref, joint_ref, inner_q, inner_b, outer_q, outer_b,
    incoming_ref, halo_ref, sent, got, node_send, node_recv, halo_send, halo_recv,
):
    grp = lax.axis_index("grp")
    pos = lax.axis_index("leaf")
    inner = inner_q.shape[0]
    outer = outer_q.shape[0]
    me = grp * leaves + pos
    count = groups * leaves
    right = lax.rem(me + 1, count)
    left = lax.rem(me + count - 1, count)
    right_id = (right // leaves, lax.rem(right, leaves))
    left_id = (left // leaves, lax.rem(left, leaves))
    levels = []
    for k in range(inner):
        bit = lax.rem(pos // (1 << k), 2)
        levels.append((bit, (grp, pos + (1 - 2 * bit) * (1 << k)), inner_q, inner_b, k))
    for k in range(outer):
        bit = lax.rem(grp // (1 << k), 2)
        levels.append((bit, (grp + (1 - 2 * bit) * (1 << k), pos), outer_q, outer_b, k))

    barrier = pltpu.get_barrier_semaphore()
    for who in [left_id, right_id] + [lv[1] for lv in levels]:
        pl.semaphore_signal(barrier, inc=1, device_id=who, device_id_type=MESH)
    pl.semaphore_wait(barrier, 2 + len(levels))

    last = joint_ref.shape[1] - leaf
    halos = [
        pltpu.make_async_remote_copy(
            src_ref=joint_ref.at[:, pl.ds(last, leaf)], dst_ref=halo_ref.at[0],
            send_sem=halo_send.at[0], recv_sem=halo_recv.at[0], device_id=right_id, device_id_type=MESH,
        ),
        pltpu.make_async_remote_copy(
            src_ref=joint_ref.at[:, pl.ds(0, leaf)], dst_ref=halo_ref.at[1],
            send_sem=halo_send.at[1], recv_sem=halo_recv.at[1], device_id=left_id, device_id_type=MESH,
        ),
    ]

    def coupled(n):
        bit, _, _, b_ref, k = levels[n]
        other = got[n]
        mat = b_ref[k]
        return fold(jnp.where(bit == 0, nt(other, mat), nn(other, mat)))

    records = []
    for n, (bit, partner, q_ref, b_ref, k) in enumerate(levels):
        source = node_ref if n == 0 else sent.at[n]
        copy = pltpu.make_async_remote_copy(
            src_ref=source, dst_ref=got.at[n], send_sem=node_send.at[n], recv_sem=node_recv.at[n],
            device_id=partner, device_id_type=MESH,
        )
        copy.start()
        if n == 0:
            for halo in halos:
                halo.start()
        else:
            records.append(coupled(n - 1))
        final = n == len(levels) - 1
        if not final:
            mine = nn(source[...], q_ref[k, bit])
        copy.wait()
        if not final:
            sent[n + 1] = split(fold(mine + nn(got[n], q_ref[k, 1 - bit])))
    incoming = coupled(len(levels) - 1)
    for n in reversed(range(len(levels) - 1)):
        bit, _, q_ref, _, k = levels[n]
        incoming = records[n] + fold(nt(split(incoming), q_ref[k, bit]))
    incoming_ref[...] = incoming
    for halo in halos:
        halo.wait()


def near_kernel(near_ref, joint_ref, halo_ref, out_ref, source, target):
    leaf_dev = near_ref.shape[0]
    rows = joint_ref.shape[0]
    leaf = halo_ref.shape[2]
    nrhs = out_ref.shape[0]
    dim = rows - nrhs
    tile = min(leaf, 256)
    scale = 2.0 / dim * math.log2(math.e)

    def parts(pts):
        wide = pts.astype(f32)
        sq = jnp.sum(wide * wide, axis=0, keepdims=True)
        high = sq.astype(bf16).astype(f32)
        mid = (sq - high).astype(bf16).astype(f32)
        low = sq - high - mid
        row = lax.broadcasted_iota(jnp.int32, (128 - dim, pts.shape[1]), 0)

        def extra(first, second):
            ones = jnp.where(jnp.logical_and(row >= second, row < second + 3), 1.0, 0.0)
            return jnp.where(row == first, -high, jnp.where(row == first + 1, -mid, jnp.where(row == first + 2, -low, ones)))

        return wide, extra

    def put_source(slot, pts):
        wide, extra = parts(pts)
        source[slot] = jnp.concatenate([2.0 * wide, extra(0, 3)], axis=0).T.astype(bf16)

    put_source(0, halo_ref[0, :dim, :])
    put_source(leaf_dev + 1, halo_ref[1, :dim, :])

    @pl.loop(0, leaf_dev)
    def _(i):
        pts = joint_ref[:dim, pl.ds(pl.multiple_of(i * leaf, leaf), leaf)]
        put_source(i + 1, pts)
        wide, extra = parts(pts)
        target[i] = jnp.concatenate([wide, extra(3, 0)], axis=0).astype(bf16)

    def block(i, slot, values):
        acc = jnp.zeros((nrhs, leaf), f32)
        for t in range(leaf // tile):
            power = nn(source[slot, t * tile : (t + 1) * tile, :], target[i])
            kern = jnp.exp2(power * scale).astype(bf16)
            acc += nn(values(t), kern)
        return acc

    def own(j):
        def values(t):
            return joint_ref[dim:, pl.ds(pl.multiple_of(j * leaf + t * tile, tile), tile)]

        return values

    def edge(side):
        return lambda t: halo_ref[side, dim:, t * tile : (t + 1) * tile]

    def flag(i, column):
        return jnp.where(near_ref[i, column] >= 0, 1.0, 0.0).astype(f32)

    @pl.loop(0, leaf_dev)
    def _(i):
        out_ref[:, pl.ds(pl.multiple_of(i * leaf, leaf), leaf)] = block(i, i + 1, own(i))

    @pl.loop(0, leaf_dev - 1)
    def _(i):
        here = pl.ds(pl.multiple_of(i * leaf, leaf), leaf)
        out_ref[:, here] += flag(i, 2) * block(i, i + 2, own(i + 1))
        there = pl.ds(pl.multiple_of(i * leaf + leaf, leaf), leaf)
        out_ref[:, there] += flag(i + 1, 1) * block(i + 1, i + 1, own(i))

    out_ref[:, :leaf] += flag(0, 1) * block(0, 0, edge(0))
    out_ref[:, (leaf_dev - 1) * leaf :] += flag(leaf_dev - 1, 2) * block(leaf_dev - 1, leaf_dev + 1, edge(1))


def total_kernel(
    groups, leaves, incoming_ref, trans_ref, bases_ref, near_ref, direction_ref, residual_ref,
    image_ref, sums_ref, first, second, first_send, first_recv, second_send, second_recv,
):
    grp = lax.axis_index("grp")
    pos = lax.axis_index("leaf")
    barrier = pltpu.get_barrier_semaphore()
    for o in range(1, leaves):
        pl.semaphore_signal(barrier, inc=1, device_id=(grp, lax.rem(pos + o, leaves)), device_id_type=MESH)
    for o in range(1, groups):
        pl.semaphore_signal(barrier, inc=1, device_id=(lax.rem(grp + o, groups), pos), device_id_type=MESH)

    leaf_dev, leaf = bases_ref.shape[:2]
    nrhs = direction_ref.shape[0]
    stacked = split(incoming_ref[...])
    sums = [jnp.zeros((nrhs, 128), f32)] * 4

    def narrow(value):
        out = value[:, :128]
        for c in range(1, value.shape[1] // 128):
            out += value[:, c * 128 : (c + 1) * 128]
        return out

    for i in range(leaf_dev):
        cols = slice(i * leaf, (i + 1) * leaf)
        leaf_in = fold(nt(stacked, trans_ref[i])).astype(bf16)
        way = direction_ref[:, cols]
        rest = residual_ref[:, cols]
        image = ridge * way + near_ref[:, cols] + nt(leaf_in, bases_ref[i])
        image_ref[:, cols] = image
        terms = (rest * rest, way * image, rest * image, image * image)
        sums = [s + narrow(t) for s, t in zip(sums, terms)]
    rows = [jnp.sum(s.T, axis=0, keepdims=True) for s in sums]
    first[pos] = jnp.concatenate(rows + [jnp.zeros((4, nrhs), f32)], axis=0)
    pl.semaphore_wait(barrier, leaves - 1 + groups - 1)

    def exchange(slots, mine, count, send, recv, where):
        def copy(o, slot):
            return pltpu.make_async_remote_copy(
                src_ref=slots.at[slot], dst_ref=slots.at[slot], send_sem=send.at[o], recv_sem=recv.at[slot],
                device_id=where(lax.rem(mine + o, count)), device_id_type=MESH,
            )

        for o in range(1, count):
            copy(o, mine).start()
        for o in range(1, count):
            copy(o, lax.rem(mine + o, count)).wait_recv()
        for o in range(1, count):
            copy(o, mine).wait_send()
        out = slots[0]
        for s in range(1, count):
            out += slots[s]
        return out

    second[grp] = exchange(first, pos, leaves, first_send, first_recv, lambda t: (grp, t))
    sums_ref[...] = exchange(second, grp, groups, second_send, second_recv, lambda t: (t, pos))


def body(groups, leaves, points, solution, residual, direction, near, bases, leaf_transfer,
         inner_transfer, inner_coupling, outer_transfer, outer_coupling):
    leaf_dev = near.shape[0]
    leaf, rank = bases.shape[1:]
    count, dim = points.shape
    nrhs = direction.shape[1]
    rows = dim + nrhs
    levels = inner_transfer.shape[0] + outer_transfer.shape[0]
    p, x, r, d = points.T, solution.T, residual.T, direction.T
    joint, node = pl.pallas_call(
        upward_kernel,
        grid=(leaf_dev,),
        in_specs=[
            pl.BlockSpec((dim, leaf), lambda i: (0, i)),
            pl.BlockSpec((nrhs, leaf), lambda i: (0, i)),
            pl.BlockSpec((1, leaf, rank), lambda i: (i, 0, 0)),
            pl.BlockSpec((1, rank, rank), lambda i: (i, 0, 0)),
        ],
        out_specs=[
            pl.BlockSpec((rows, leaf), lambda i: (0, i)),
            pl.BlockSpec((2 * nrhs, rank), lambda i: (0, 0)),
        ],
        out_shape=[
            jax.ShapeDtypeStruct((rows, count), bf16),
            jax.ShapeDtypeStruct((2 * nrhs, rank), bf16),
        ],
        scratch_shapes=[pltpu.VMEM((nrhs, rank), f32)],
        name="upward",
    )(p, d, bases, leaf_transfer)
    incoming, halo = pl.pallas_call(
        functools.partial(tree_kernel, groups, leaves, leaf),
        in_specs=[vmem] * 6,
        out_specs=[vmem] * 2,
        out_shape=[
            jax.ShapeDtypeStruct((nrhs, rank), f32),
            jax.ShapeDtypeStruct((2, rows, leaf), bf16),
        ],
        scratch_shapes=[
            pltpu.VMEM((levels, 2 * nrhs, rank), bf16),
            pltpu.VMEM((levels, 2 * nrhs, rank), bf16),
            pltpu.SemaphoreType.DMA((levels,)),
            pltpu.SemaphoreType.DMA((levels,)),
            pltpu.SemaphoreType.DMA((2,)),
            pltpu.SemaphoreType.DMA((2,)),
        ],
        compiler_params=pltpu.CompilerParams(collective_id=0, has_side_effects=True),
        name="tree",
    )(node, joint, inner_transfer, inner_coupling, outer_transfer, outer_coupling)
    near_term = pl.pallas_call(
        near_kernel,
        in_specs=[smem, vmem, vmem],
        out_specs=vmem,
        out_shape=jax.ShapeDtypeStruct((nrhs, count), f32),
        scratch_shapes=[
            pltpu.VMEM((leaf_dev + 2, leaf, 128), bf16),
            pltpu.VMEM((leaf_dev, 128, leaf), bf16),
        ],
        name="near",
    )(near, joint, halo)
    image, sums = pl.pallas_call(
        functools.partial(total_kernel, groups, leaves),
        in_specs=[vmem] * 6,
        out_specs=[vmem] * 2,
        out_shape=[
            jax.ShapeDtypeStruct((nrhs, count), f32),
            jax.ShapeDtypeStruct((8, nrhs), f32),
        ],
        scratch_shapes=[
            pltpu.VMEM((leaves, 8, nrhs), f32),
            pltpu.VMEM((groups, 8, nrhs), f32),
            pltpu.SemaphoreType.DMA((leaves,)),
            pltpu.SemaphoreType.DMA((leaves,)),
            pltpu.SemaphoreType.DMA((groups,)),
            pltpu.SemaphoreType.DMA((groups,)),
        ],
        compiler_params=pltpu.CompilerParams(collective_id=1, has_side_effects=True),
        name="total",
    )(incoming, leaf_transfer, bases, near_term, d, r)
    rr, pq, rq, qq = sums[0], sums[1], sums[2], sums[3]
    alpha = rr / pq
    fresh = rr - 2.0 * alpha * rq + alpha * alpha * qq
    beta = fresh / rr
    new_residual = r - alpha[:, None] * image
    return (
        (x + alpha[:, None] * d).T,
        new_residual.T,
        (new_residual + beta[:, None] * d).T,
    )


def solution(mesh):
    both = ("grp", "leaf")
    flat = P(both, None)
    deep = P(both, None, None)
    return jax.shard_map(
        functools.partial(body, mesh.shape["grp"], mesh.shape["leaf"]),
        mesh=mesh,
        in_specs=(flat, flat, flat, flat, flat, deep, deep, P(), P(), P(), P()),
        out_specs=(flat, flat, flat),
        check_vma=False,
    )
```

```python
import functools
import math

import jax
import jax.numpy as jnp
from jax import lax
from jax.experimental import pallas as pl
from jax.experimental.pallas import tpu as pltpu
from jax.sharding import PartitionSpec as P

MESH = pl.DeviceIdType.MESH
ridge = 2.0
f32 = jnp.float32
bf16 = jnp.bfloat16
vmem = pl.BlockSpec(memory_space=pltpu.VMEM)
smem = pl.BlockSpec(memory_space=pltpu.SMEM)


def nn(a, b):
    return jnp.dot(a, b, preferred_element_type=f32)


def nt(a, b):
    return lax.dot_general(a, b, (((1,), (1,)), ((), ())), preferred_element_type=f32)


def split(value):
    high = value.astype(bf16)
    low = (value - high.astype(f32)).astype(bf16)
    return jnp.concatenate([high, low], axis=0)


def fold(stacked):
    half = stacked.shape[0] // 2
    return stacked[:half] + stacked[half:]


def upward_kernel(points_ref, direction_ref, bases_ref, trans_ref, joint_ref, node_ref, acc):
    step = pl.program_id(0)
    dim = points_ref.shape[0]
    packed = direction_ref[...].astype(bf16)
    joint_ref[:dim, :] = points_ref[...]
    joint_ref[dim:, :] = packed
    term = fold(nn(split(nn(packed, bases_ref[0])), trans_ref[0]))

    @pl.when(step == 0)
    def _():
        acc[...] = term

    @pl.when(step > 0)
    def _():
        acc[...] += term

    @pl.when(step == pl.num_programs(0) - 1)
    def _():
        node_ref[...] = split(acc[...])


def step_kernel(
    groups, leaves, near_ref, node_ref, joint_ref, inner_q, inner_b, outer_q, outer_b,
    trans_hbm, bases_hbm, direction_hbm, residual_hbm, image_ref, sums_ref,
    sent, got, halo_ref, source, target, trans_ref, bases_ref, direction_ref, residual_ref, first, second,
    node_send, node_recv, halo_send, halo_recv, first_send, first_recv, second_send, second_recv, load_sem,
):
    loads = [
        pltpu.make_async_copy(src, dst, load_sem.at[n])
        for n, (src, dst) in enumerate(
            [(trans_hbm, trans_ref), (bases_hbm, bases_ref), (direction_hbm, direction_ref), (residual_hbm, residual_ref)]
        )
    ]
    for load in loads:
        load.start()
    grp = lax.axis_index("grp")
    pos = lax.axis_index("leaf")
    inner = inner_q.shape[0]
    outer = outer_q.shape[0]
    me = grp * leaves + pos
    count = groups * leaves
    right = lax.rem(me + 1, count)
    left = lax.rem(me + count - 1, count)
    right_id = (right // leaves, lax.rem(right, leaves))
    left_id = (left // leaves, lax.rem(left, leaves))
    levels = []
    for k in range(inner):
        bit = lax.rem(pos // (1 << k), 2)
        levels.append((bit, (grp, pos + (1 - 2 * bit) * (1 << k)), inner_q, inner_b, k))
    for k in range(outer):
        bit = lax.rem(grp // (1 << k), 2)
        levels.append((bit, (grp + (1 - 2 * bit) * (1 << k), pos), outer_q, outer_b, k))

    barrier = pltpu.get_barrier_semaphore()
    greeted = [left_id, right_id]
    greeted += [(grp, lax.rem(pos + o, leaves)) for o in range(1, leaves)]
    greeted += [(lax.rem(grp + o, groups), pos) for o in range(1, groups)]
    for who in greeted:
        pl.semaphore_signal(barrier, inc=1, device_id=who, device_id_type=MESH)

    leaf_dev, leaf = bases_ref.shape[:2]
    nrhs = image_ref.shape[0]
    dim = joint_ref.shape[0] - nrhs
    tile = min(leaf, 256)
    scale = 2.0 / dim * math.log2(math.e)

    def parts(pts):
        wide = pts.astype(f32)
        sq = jnp.sum(wide * wide, axis=0, keepdims=True)
        high = sq.astype(bf16).astype(f32)
        mid = (sq - high).astype(bf16).astype(f32)
        low = sq - high - mid
        row = lax.broadcasted_iota(jnp.int32, (128 - dim, pts.shape[1]), 0)

        def extra(first, second):
            ones = jnp.where(jnp.logical_and(row >= second, row < second + 3), 1.0, 0.0)
            return jnp.where(row == first, -high, jnp.where(row == first + 1, -mid, jnp.where(row == first + 2, -low, ones)))

        return wide, extra

    def put_source(slot, wide, extra):
        source[slot] = jnp.concatenate([2.0 * wide, extra(0, 3)], axis=0).T.astype(bf16)

    for i in range(leaf_dev):
        wide, extra = parts(joint_ref[:dim, i * leaf : (i + 1) * leaf])
        put_source(i + 1, wide, extra)
        target[i] = jnp.concatenate([wide, extra(3, 0)], axis=0).astype(bf16)

    def block(i, slot, values):
        acc = jnp.zeros((nrhs, leaf), f32)
        for t in range(leaf // tile):
            power = nn(source[slot, t * tile : (t + 1) * tile, :], target[i])
            kern = jnp.exp2(power * scale).astype(bf16)
            acc += nn(values(t), kern)
        return acc

    def own(j):
        return lambda t: joint_ref[dim:, j * leaf + t * tile : j * leaf + (t + 1) * tile]

    def edge(side):
        return lambda t: halo_ref[side, dim:, t * tile : (t + 1) * tile]

    def flagged(i, column, slot, values):
        flag = jnp.where(near_ref[i, column] >= 0, 1.0, 0.0).astype(f32)
        image_ref[:, i * leaf : (i + 1) * leaf] += flag * block(i, slot, values)

    def itself(i):
        image_ref[:, i * leaf : (i + 1) * leaf] = block(i, i + 1, own(i))

    jobs = [functools.partial(itself, i) for i in range(leaf_dev)]
    for i in range(leaf_dev - 1):
        jobs.append(functools.partial(flagged, i, 2, i + 2, own(i + 1)))
        jobs.append(functools.partial(flagged, i + 1, 1, i + 1, own(i)))

    pl.semaphore_wait(barrier, len(greeted))

    last = joint_ref.shape[1] - leaf
    halos = [
        pltpu.make_async_remote_copy(
            src_ref=joint_ref.at[:, pl.ds(last, leaf)], dst_ref=halo_ref.at[0],
            send_sem=halo_send.at[0], recv_sem=halo_recv.at[0], device_id=right_id, device_id_type=MESH,
        ),
        pltpu.make_async_remote_copy(
            src_ref=joint_ref.at[:, pl.ds(0, leaf)], dst_ref=halo_ref.at[1],
            send_sem=halo_send.at[1], recv_sem=halo_recv.at[1], device_id=left_id, device_id_type=MESH,
        ),
    ]

    def coupled(n):
        bit, _, _, b_ref, k = levels[n]
        other = got[n]
        mat = b_ref[k]
        return fold(jnp.where(bit == 0, nt(other, mat), nn(other, mat)))

    records = []
    for n, (bit, partner, q_ref, b_ref, k) in enumerate(levels):
        holder = node_ref if n == 0 else sent.at[n]
        copy = pltpu.make_async_remote_copy(
            src_ref=holder, dst_ref=got.at[n], send_sem=node_send.at[n], recv_sem=node_recv.at[n],
            device_id=partner, device_id_type=MESH,
        )
        copy.start()
        if n == inner:
            for halo in halos:
                halo.start()
        if n > 0:
            records.append(coupled(n - 1))
        final = n == len(levels) - 1
        if not final:
            mine = nn(holder[...], q_ref[k, bit])
        for job in jobs[n * len(jobs) // len(levels) : (n + 1) * len(jobs) // len(levels)]:
            job()
        copy.wait()
        if not final:
            sent[n + 1] = split(fold(mine + nn(got[n], q_ref[k, 1 - bit])))
    incoming = coupled(len(levels) - 1)
    for n in reversed(range(len(levels) - 1)):
        bit, _, q_ref, _, k = levels[n]
        incoming = records[n] + fold(nt(split(incoming), q_ref[k, bit]))

    stacked = split(incoming)
    for load in loads:
        load.wait()
    for i in range(leaf_dev):
        cols = slice(i * leaf, (i + 1) * leaf)
        leaf_in = fold(nt(stacked, trans_ref[i])).astype(bf16)
        image_ref[:, cols] += ridge * direction_ref[:, cols] + nt(leaf_in, bases_ref[i])

    for side, (i, column, slot) in enumerate([(0, 1, 0), (leaf_dev - 1, 2, leaf_dev + 1)]):
        halos[side].wait()
        put_source(slot, *parts(halo_ref[side, :dim, :]))
        flagged(i, column, slot, edge(side))

    sums = [jnp.zeros((nrhs, 128), f32)] * 4

    def narrow(value):
        out = value[:, :128]
        for c in range(1, value.shape[1] // 128):
            out += value[:, c * 128 : (c + 1) * 128]
        return out

    for i in range(leaf_dev):
        cols = slice(i * leaf, (i + 1) * leaf)
        way = direction_ref[:, cols]
        rest = residual_ref[:, cols]
        image = image_ref[:, cols]
        terms = (rest * rest, way * image, rest * image, image * image)
        sums = [s + narrow(t) for s, t in zip(sums, terms)]
    rows = [jnp.sum(s.T, axis=0, keepdims=True) for s in sums]
    first[pos] = jnp.concatenate(rows + [jnp.zeros((4, nrhs), f32)], axis=0)

    def exchange(slots, mine, count, send, recv, where):
        def copy(o, slot):
            return pltpu.make_async_remote_copy(
                src_ref=slots.at[slot], dst_ref=slots.at[slot], send_sem=send.at[o], recv_sem=recv.at[slot],
                device_id=where(lax.rem(mine + o, count)), device_id_type=MESH,
            )

        for o in range(1, count):
            copy(o, mine).start()
        for o in range(1, count):
            copy(o, lax.rem(mine + o, count)).wait_recv()
        for o in range(1, count):
            copy(o, mine).wait_send()
        out = slots[0]
        for s in range(1, count):
            out += slots[s]
        return out

    second[grp] = exchange(first, pos, leaves, first_send, first_recv, lambda t: (grp, t))
    sums_ref[...] = exchange(second, grp, groups, second_send, second_recv, lambda t: (t, pos))


def update_kernel(sums_ref, x_ref, r_ref, d_ref, image_ref, new_x, new_r, new_d):
    rr, pq, rq, qq = [sums_ref[c : c + 1, :] for c in range(4)]
    alpha = rr / pq
    fresh = rr - 2.0 * alpha * rq + alpha * alpha * qq
    nrhs = x_ref.shape[0]
    square = (nrhs, nrhs)
    diagonal = lax.broadcasted_iota(jnp.int32, square, 0) == lax.broadcasted_iota(jnp.int32, square, 1)

    def column(row):
        return jnp.sum(jnp.where(diagonal, jnp.broadcast_to(row, square), 0.0), axis=1, keepdims=True)

    step, blend = column(alpha), column(fresh / rr)
    way = d_ref[...]
    new_x[...] = x_ref[...] + step * way
    rest = r_ref[...] - step * image_ref[...]
    new_r[...] = rest
    new_d[...] = rest + blend * way


def body(groups, leaves, points, solution, residual, direction, near, bases, leaf_transfer,
         inner_transfer, inner_coupling, outer_transfer, outer_coupling):
    leaf_dev = near.shape[0]
    leaf, rank = bases.shape[1:]
    count, dim = points.shape
    nrhs = direction.shape[1]
    rows = dim + nrhs
    levels = inner_transfer.shape[0] + outer_transfer.shape[0]
    p, x, r, d = points.T, solution.T, residual.T, direction.T
    joint, node = pl.pallas_call(
        upward_kernel,
        grid=(leaf_dev,),
        in_specs=[
            pl.BlockSpec((dim, leaf), lambda i: (0, i)),
            pl.BlockSpec((nrhs, leaf), lambda i: (0, i)),
            pl.BlockSpec((1, leaf, rank), lambda i: (i, 0, 0)),
            pl.BlockSpec((1, rank, rank), lambda i: (i, 0, 0)),
        ],
        out_specs=[
            pl.BlockSpec((rows, leaf), lambda i: (0, i)),
            pl.BlockSpec((2 * nrhs, rank), lambda i: (0, 0)),
        ],
        out_shape=[
            jax.ShapeDtypeStruct((rows, count), bf16),
            jax.ShapeDtypeStruct((2 * nrhs, rank), bf16),
        ],
        scratch_shapes=[pltpu.VMEM((nrhs, rank), f32)],
        name="upward",
    )(p, d, bases, leaf_transfer)
    anywhere = pl.BlockSpec(memory_space=pl.ANY)
    sems = pltpu.SemaphoreType.DMA
    image, sums = pl.pallas_call(
        functools.partial(step_kernel, groups, leaves),
        in_specs=[smem] + [vmem] * 6 + [anywhere] * 4,
        out_specs=[vmem] * 2,
        out_shape=[
            jax.ShapeDtypeStruct((nrhs, count), f32),
            jax.ShapeDtypeStruct((8, nrhs), f32),
        ],
        scratch_shapes=[
            pltpu.VMEM((levels, 2 * nrhs, rank), bf16),
            pltpu.VMEM((levels, 2 * nrhs, rank), bf16),
            pltpu.VMEM((2, rows, leaf), bf16),
            pltpu.VMEM((leaf_dev + 2, leaf, 128), bf16),
            pltpu.VMEM((leaf_dev, 128, leaf), bf16),
            pltpu.VMEM(leaf_transfer.shape, bf16),
            pltpu.VMEM(bases.shape, bf16),
            pltpu.VMEM((nrhs, count), f32),
            pltpu.VMEM((nrhs, count), f32),
            pltpu.VMEM((leaves, 8, nrhs), f32),
            pltpu.VMEM((groups, 8, nrhs), f32),
            sems((levels,)), sems((levels,)), sems((2,)), sems((2,)),
            sems((leaves,)), sems((leaves,)), sems((groups,)), sems((groups,)), sems((4,)),
        ],
        compiler_params=pltpu.CompilerParams(collective_id=0, has_side_effects=True),
        name="step",
    )(near, node, joint, inner_transfer, inner_coupling, outer_transfer, outer_coupling, leaf_transfer, bases, d, r)
    wide = pl.BlockSpec((nrhs, leaf), lambda i: (0, i))
    outs = pl.pallas_call(
        update_kernel,
        grid=(leaf_dev,),
        in_specs=[pl.BlockSpec((8, nrhs), lambda i: (0, 0))] + [wide] * 4,
        out_specs=[wide] * 3,
        out_shape=[jax.ShapeDtypeStruct((nrhs, count), f32)] * 3,
        name="update",
    )(sums, x, r, d, image)
    return tuple(out.T for out in outs)


def solution(mesh):
    both = ("grp", "leaf")
    flat = P(both, None)
    deep = P(both, None, None)
    return jax.shard_map(
        functools.partial(body, mesh.shape["grp"], mesh.shape["leaf"]),
        mesh=mesh,
        in_specs=(flat, flat, flat, flat, flat, deep, deep, P(), P(), P(), P()),
        out_specs=(flat, flat, flat),
        check_vma=False,
    )
```

```python
import functools
import math

import jax
import jax.numpy as jnp
from jax import lax
from jax.experimental import pallas as pl
from jax.experimental.pallas import tpu as pltpu
from jax.sharding import PartitionSpec as P

MESH = pl.DeviceIdType.MESH
ridge = 2.0
f32 = jnp.float32
bf16 = jnp.bfloat16
vmem = pl.BlockSpec(memory_space=pltpu.VMEM)
smem = pl.BlockSpec(memory_space=pltpu.SMEM)


def nn(a, b):
    return jnp.dot(a, b, preferred_element_type=f32)


def nt(a, b):
    return lax.dot_general(a, b, (((1,), (1,)), ((), ())), preferred_element_type=f32)


def split(value):
    high = value.astype(bf16)
    low = (value - high.astype(f32)).astype(bf16)
    return jnp.concatenate([high, low], axis=0)


def fold(stacked):
    half = stacked.shape[0] // 2
    return stacked[:half] + stacked[half:]


def step_kernel(
    groups, leaves, near_ref, inner_q, inner_b, outer_q, outer_b,
    points_hbm, trans_hbm, bases_hbm, direction_hbm, residual_hbm, image_ref, sums_ref, joint_ref, sent, got, halo_ref, source, target, trans_ref, bases_ref, direction_ref, residual_ref, first, second,
    node_send, node_recv, halo_send, halo_recv, first_send, first_recv, second_send, second_recv, load_sem,
):
    leaf_dev, leaf = bases_ref.shape[:2]
    nrhs = image_ref.shape[0]
    dim = joint_ref.shape[0] - nrhs
    pairs = [(direction_hbm, direction_ref), (trans_hbm, trans_ref)]
    pairs += [(bases_hbm.at[i], bases_ref.at[i]) for i in range(leaf_dev)]
    pairs += [(points_hbm, joint_ref.at[pl.ds(0, dim), :]), (residual_hbm, residual_ref)]
    loads = [pltpu.make_async_copy(src, dst, load_sem.at[n]) for n, (src, dst) in enumerate(pairs)]
    for load in loads:
        load.start()
    grp = lax.axis_index("grp")
    pos = lax.axis_index("leaf")
    inner = inner_q.shape[0]
    outer = outer_q.shape[0]
    me = grp * leaves + pos
    count = groups * leaves
    right = lax.rem(me + 1, count)
    left = lax.rem(me + count - 1, count)
    right_id = (right // leaves, lax.rem(right, leaves))
    left_id = (left // leaves, lax.rem(left, leaves))
    levels = []
    for k in range(inner):
        bit = lax.rem(pos // (1 << k), 2)
        levels.append((bit, (grp, pos + (1 - 2 * bit) * (1 << k)), inner_q, inner_b, k))
    for k in range(outer):
        bit = lax.rem(grp // (1 << k), 2)
        levels.append((bit, (grp + (1 - 2 * bit) * (1 << k), pos), outer_q, outer_b, k))

    barrier = pltpu.get_barrier_semaphore()
    greeted = [left_id, right_id]
    greeted += [(grp, lax.rem(pos + o, leaves)) for o in range(1, leaves)]
    greeted += [(lax.rem(grp + o, groups), pos) for o in range(1, groups)]
    for who in greeted:
        pl.semaphore_signal(barrier, inc=1, device_id=who, device_id_type=MESH)

    loads[0].wait()
    joint_ref[dim:, :] = direction_ref[...].astype(bf16)
    loads[1].wait()
    node = None
    for i in range(leaf_dev):
        loads[2 + i].wait()
        skel = nn(joint_ref[dim:, i * leaf : (i + 1) * leaf], bases_ref[i])
        term = nn(split(skel), trans_ref[i])
        node = term if node is None else node + term
    sent[0] = split(fold(node))
    loads[-2].wait()

    tile = min(leaf, 256)
    scale = 2.0 / dim * math.log2(math.e)

    def parts(pts):
        wide = pts.astype(f32)
        sq = jnp.sum(wide * wide, axis=0, keepdims=True)
        high = sq.astype(bf16).astype(f32)
        mid = (sq - high).astype(bf16).astype(f32)
        low = sq - high - mid
        row = lax.broadcasted_iota(jnp.int32, (128 - dim, pts.shape[1]), 0)

        def extra(first, second):
            ones = jnp.where(jnp.logical_and(row >= second, row < second + 3), 1.0, 0.0)
            return jnp.where(row == first, -high, jnp.where(row == first + 1, -mid, jnp.where(row == first + 2, -low, ones)))

        return wide, extra

    def put_source(slot, wide, extra):
        source[slot] = jnp.concatenate([2.0 * wide, extra(0, 3)], axis=0).T.astype(bf16)

    def block(i, slot, values):
        acc = jnp.zeros((nrhs, leaf), f32)
        for t in range(leaf // tile):
            power = nn(source[slot, t * tile : (t + 1) * tile, :], target[i])
            kern = jnp.exp2(power * scale).astype(bf16)
            acc += nn(values(t), kern)
        return acc

    def own(j):
        return lambda t: joint_ref[dim:, j * leaf + t * tile : j * leaf + (t + 1) * tile]

    def edge(side):
        return lambda t: halo_ref[side, dim:, t * tile : (t + 1) * tile]

    def flagged(i, column, slot, values):
        flag = jnp.where(near_ref[i, column] >= 0, 1.0, 0.0).astype(f32)
        image_ref[:, i * leaf : (i + 1) * leaf] += flag * block(i, slot, values)

    def itself(i):
        wide, extra = parts(joint_ref[:dim, i * leaf : (i + 1) * leaf])
        put_source(i + 1, wide, extra)
        target[i] = jnp.concatenate([wide, extra(3, 0)], axis=0).astype(bf16)
        image_ref[:, i * leaf : (i + 1) * leaf] = block(i, i + 1, own(i))

    def beside(i):
        here = jnp.where(near_ref[i, 2] >= 0, 1.0, 0.0).astype(f32)
        there = jnp.where(near_ref[i + 1, 1] >= 0, 1.0, 0.0).astype(f32)
        mine = joint_ref[dim:, i * leaf : (i + 1) * leaf]
        values = own(i + 1)
        acc = jnp.zeros((nrhs, leaf), f32)
        for t in range(leaf // tile):
            power = nn(source[i + 2, t * tile : (t + 1) * tile, :], target[i])
            kern = jnp.exp2(power * scale).astype(bf16)
            acc += nn(values(t), kern)
            cols = slice((i + 1) * leaf + t * tile, (i + 1) * leaf + (t + 1) * tile)
            image_ref[:, cols] += there * nt(mine, kern)
        image_ref[:, i * leaf : (i + 1) * leaf] += here * acc

    jobs = [functools.partial(itself, i) for i in range(leaf_dev)]
    jobs += [functools.partial(beside, i) for i in range(leaf_dev - 1)]

    pl.semaphore_wait(barrier, len(greeted))

    last = joint_ref.shape[1] - leaf
    halos = [
        pltpu.make_async_remote_copy(
            src_ref=joint_ref.at[:, pl.ds(last, leaf)], dst_ref=halo_ref.at[0],
            send_sem=halo_send.at[0], recv_sem=halo_recv.at[0], device_id=right_id, device_id_type=MESH,
        ),
        pltpu.make_async_remote_copy(
            src_ref=joint_ref.at[:, pl.ds(0, leaf)], dst_ref=halo_ref.at[1],
            send_sem=halo_send.at[1], recv_sem=halo_recv.at[1], device_id=left_id, device_id_type=MESH,
        ),
    ]

    def coupled(n):
        bit, _, _, b_ref, k = levels[n]
        other = got[n]
        mat = b_ref[k]
        return fold(jnp.where(bit == 0, nt(other, mat), nn(other, mat)))

    records = []
    for n, (bit, partner, q_ref, b_ref, k) in enumerate(levels):
        holder = sent.at[n]
        copy = pltpu.make_async_remote_copy(
            src_ref=holder, dst_ref=got.at[n], send_sem=node_send.at[n], recv_sem=node_recv.at[n],
            device_id=partner, device_id_type=MESH,
        )
        copy.start()
        if n == inner:
            for halo in halos:
                halo.start()
        if n > 0:
            records.append(coupled(n - 1))
        final = n == len(levels) - 1
        if not final:
            mine = nn(holder[...], q_ref[k, bit])
        for job in jobs[n * len(jobs) // len(levels) : (n + 1) * len(jobs) // len(levels)]:
            job()
        copy.wait()
        if not final:
            sent[n + 1] = split(fold(mine + nn(got[n], q_ref[k, 1 - bit])))
    incoming = coupled(len(levels) - 1)
    for n in reversed(range(len(levels) - 1)):
        bit, _, q_ref, _, k = levels[n]
        incoming = records[n] + fold(nt(split(incoming), q_ref[k, bit]))

    stacked = split(incoming)
    loads[-1].wait()
    for i in range(leaf_dev):
        cols = slice(i * leaf, (i + 1) * leaf)
        leaf_in = fold(nt(stacked, trans_ref[i])).astype(bf16)
        image_ref[:, cols] += ridge * direction_ref[:, cols] + nt(leaf_in, bases_ref[i])

    for side, (i, column, slot) in enumerate([(0, 1, 0), (leaf_dev - 1, 2, leaf_dev + 1)]):
        halos[side].wait()
        put_source(slot, *parts(halo_ref[side, :dim, :]))
        flagged(i, column, slot, edge(side))

    sums = [jnp.zeros((nrhs, 128), f32)] * 4

    def narrow(value):
        out = value[:, :128]
        for c in range(1, value.shape[1] // 128):
            out += value[:, c * 128 : (c + 1) * 128]
        return out

    for i in range(leaf_dev):
        cols = slice(i * leaf, (i + 1) * leaf)
        way = direction_ref[:, cols]
        rest = residual_ref[:, cols]
        image = image_ref[:, cols]
        terms = (rest * rest, way * image, rest * image, image * image)
        sums = [s + narrow(t) for s, t in zip(sums, terms)]
    rows = [jnp.sum(s.T, axis=0, keepdims=True) for s in sums]
    first[pos] = jnp.concatenate(rows + [jnp.zeros((4, nrhs), f32)], axis=0)

    def exchange(slots, mine, count, send, recv, where):
        def copy(o, slot):
            return pltpu.make_async_remote_copy(
                src_ref=slots.at[slot], dst_ref=slots.at[slot], send_sem=send.at[o], recv_sem=recv.at[slot],
                device_id=where(lax.rem(mine + o, count)), device_id_type=MESH,
            )

        for o in range(1, count):
            copy(o, mine).start()
        for o in range(1, count):
            copy(o, lax.rem(mine + o, count)).wait_recv()
        for o in range(1, count):
            copy(o, mine).wait_send()
        out = slots[0]
        for s in range(1, count):
            out += slots[s]
        return out

    second[grp] = exchange(first, pos, leaves, first_send, first_recv, lambda t: (grp, t))
    sums_ref[...] = exchange(second, grp, groups, second_send, second_recv, lambda t: (t, pos))


def update_kernel(sums_ref, x_ref, r_ref, d_ref, image_ref, new_x, new_r, new_d):
    rr, pq, rq, qq = [sums_ref[c : c + 1, :] for c in range(4)]
    alpha = rr / pq
    fresh = rr - 2.0 * alpha * rq + alpha * alpha * qq
    nrhs = x_ref.shape[0]
    square = (nrhs, nrhs)
    diagonal = lax.broadcasted_iota(jnp.int32, square, 0) == lax.broadcasted_iota(jnp.int32, square, 1)

    def column(row):
        return jnp.sum(jnp.where(diagonal, jnp.broadcast_to(row, square), 0.0), axis=1, keepdims=True)

    step, blend = column(alpha), column(fresh / rr)
    way = d_ref[...]
    new_x[...] = x_ref[...] + step * way
    rest = r_ref[...] - step * image_ref[...]
    new_r[...] = rest
    new_d[...] = rest + blend * way


def body(groups, leaves, points, solution, residual, direction, near, bases, leaf_transfer,
         inner_transfer, inner_coupling, outer_transfer, outer_coupling):
    leaf_dev = near.shape[0]
    leaf, rank = bases.shape[1:]
    count, dim = points.shape
    nrhs = direction.shape[1]
    rows = dim + nrhs
    levels = inner_transfer.shape[0] + outer_transfer.shape[0]
    p, x, r, d = points.T, solution.T, residual.T, direction.T
    anywhere = pl.BlockSpec(memory_space=pl.ANY)
    sems = pltpu.SemaphoreType.DMA
    image, sums = pl.pallas_call(
        functools.partial(step_kernel, groups, leaves),
        in_specs=[smem] + [vmem] * 4 + [anywhere] * 5,
        out_specs=[vmem] * 2,
        out_shape=[
            jax.ShapeDtypeStruct((nrhs, count), f32),
            jax.ShapeDtypeStruct((8, nrhs), f32),
        ],
        scratch_shapes=[
            pltpu.VMEM((rows, count), bf16),
            pltpu.VMEM((levels, 2 * nrhs, rank), bf16),
            pltpu.VMEM((levels, 2 * nrhs, rank), bf16),
            pltpu.VMEM((2, rows, leaf), bf16),
            pltpu.VMEM((leaf_dev + 2, leaf, 128), bf16),
            pltpu.VMEM((leaf_dev, 128, leaf), bf16),
            pltpu.VMEM(leaf_transfer.shape, bf16),
            pltpu.VMEM(bases.shape, bf16),
            pltpu.VMEM((nrhs, count), f32),
            pltpu.VMEM((nrhs, count), f32),
            pltpu.VMEM((leaves, 8, nrhs), f32),
            pltpu.VMEM((groups, 8, nrhs), f32),
            sems((levels,)), sems((levels,)), sems((2,)), sems((2,)),
            sems((leaves,)), sems((leaves,)), sems((groups,)), sems((groups,)), sems((leaf_dev + 4,)),
        ],
        compiler_params=pltpu.CompilerParams(collective_id=0, has_side_effects=True),
        name="step",
    )(near, inner_transfer, inner_coupling, outer_transfer, outer_coupling, p, leaf_transfer, bases, d, r)
    wide = pl.BlockSpec((nrhs, leaf), lambda i: (0, i))
    outs = pl.pallas_call(
        update_kernel,
        grid=(leaf_dev,),
        in_specs=[pl.BlockSpec((8, nrhs), lambda i: (0, 0))] + [wide] * 4,
        out_specs=[wide] * 3,
        out_shape=[jax.ShapeDtypeStruct((nrhs, count), f32)] * 3,
        name="update",
    )(sums, x, r, d, image)
    return tuple(out.T for out in outs)


def solution(mesh):
    both = ("grp", "leaf")
    flat = P(both, None)
    deep = P(both, None, None)
    return jax.shard_map(
        functools.partial(body, mesh.shape["grp"], mesh.shape["leaf"]),
        mesh=mesh,
        in_specs=(flat, flat, flat, flat, flat, deep, deep, P(), P(), P(), P()),
        out_specs=(flat, flat, flat),
        check_vma=False,
    )
```

```python
import functools
import math

import jax
import jax.numpy as jnp
from jax import lax
from jax.experimental import pallas as pl
from jax.experimental.pallas import tpu as pltpu
from jax.sharding import PartitionSpec as P

MESH = pl.DeviceIdType.MESH
ridge = 2.0
f32 = jnp.float32
bf16 = jnp.bfloat16
vmem = pl.BlockSpec(memory_space=pltpu.VMEM)
smem = pl.BlockSpec(memory_space=pltpu.SMEM)


def nn(a, b):
    return jnp.dot(a, b, preferred_element_type=f32)


def nt(a, b):
    return lax.dot_general(a, b, (((1,), (1,)), ((), ())), preferred_element_type=f32)


def split(value):
    high = value.astype(bf16)
    low = (value - high.astype(f32)).astype(bf16)
    return jnp.concatenate([high, low], axis=0)


def fold(stacked):
    half = stacked.shape[0] // 2
    return stacked[:half] + stacked[half:]


def step_kernel(
    groups, leaves, near_ref, inner_q_hbm, inner_b_hbm, outer_q_hbm, outer_b_hbm,
    points_hbm, trans_hbm, bases_hbm, direction_hbm, residual_hbm, image_ref, sums_ref,
    inner_q, inner_b, outer_q, outer_b, joint_ref, sent, got, halo_ref, source, target, trans_ref, bases_ref, direction_ref, residual_ref, first, second,
    node_send, node_recv, halo_send, halo_recv, first_send, first_recv, second_send, second_recv, load_sem,
):
    leaf_dev, leaf = bases_ref.shape[:2]
    nrhs = image_ref.shape[0]
    dim = joint_ref.shape[0] - nrhs
    pairs = [(direction_hbm, direction_ref), (trans_hbm, trans_ref)]
    pairs += [(bases_hbm.at[i], bases_ref.at[i]) for i in range(leaf_dev)]
    pairs += [(points_hbm, joint_ref.at[pl.ds(0, dim), :]), (residual_hbm, residual_ref)]
    matrices = len(pairs)
    pairs += [(inner_q_hbm, inner_q), (inner_b_hbm, inner_b), (outer_q_hbm, outer_q), (outer_b_hbm, outer_b)]
    loads = [pltpu.make_async_copy(src, dst, load_sem.at[n]) for n, (src, dst) in enumerate(pairs)]
    for load in loads:
        load.start()
    grp = lax.axis_index("grp")
    pos = lax.axis_index("leaf")
    inner = inner_q.shape[0]
    outer = outer_q.shape[0]
    me = grp * leaves + pos
    count = groups * leaves
    right = lax.rem(me + 1, count)
    left = lax.rem(me + count - 1, count)
    right_id = (right // leaves, lax.rem(right, leaves))
    left_id = (left // leaves, lax.rem(left, leaves))
    levels = []
    for k in range(inner):
        bit = lax.rem(pos // (1 << k), 2)
        levels.append((bit, (grp, pos + (1 - 2 * bit) * (1 << k)), inner_q, inner_b, k))
    for k in range(outer):
        bit = lax.rem(grp // (1 << k), 2)
        levels.append((bit, (grp + (1 - 2 * bit) * (1 << k), pos), outer_q, outer_b, k))

    barrier = pltpu.get_barrier_semaphore()
    greeted = [left_id, right_id]
    greeted += [(grp, lax.rem(pos + o, leaves)) for o in range(1, leaves)]
    greeted += [(lax.rem(grp + o, groups), pos) for o in range(1, groups)]
    for who in greeted:
        pl.semaphore_signal(barrier, inc=1, device_id=who, device_id_type=MESH)

    loads[0].wait()
    joint_ref[dim:, :] = direction_ref[...].astype(bf16)
    loads[1].wait()
    node = None
    for i in range(leaf_dev):
        loads[2 + i].wait()
        skel = nn(joint_ref[dim:, i * leaf : (i + 1) * leaf], bases_ref[i])
        term = nn(split(skel), trans_ref[i])
        node = term if node is None else node + term
    sent[0] = split(fold(node))
    for load in [loads[matrices - 2]] + loads[matrices:]:
        load.wait()

    tile = min(leaf, 256)
    scale = 2.0 / dim * math.log2(math.e)

    def parts(pts):
        wide = pts.astype(f32)
        sq = jnp.sum(wide * wide, axis=0, keepdims=True)
        high = sq.astype(bf16).astype(f32)
        mid = (sq - high).astype(bf16).astype(f32)
        low = sq - high - mid
        row = lax.broadcasted_iota(jnp.int32, (128 - dim, pts.shape[1]), 0)

        def extra(first, second):
            ones = jnp.where(jnp.logical_and(row >= second, row < second + 3), 1.0, 0.0)
            return jnp.where(row == first, -high, jnp.where(row == first + 1, -mid, jnp.where(row == first + 2, -low, ones)))

        return wide, extra

    def put_source(slot, wide, extra):
        source[slot] = jnp.concatenate([2.0 * wide, extra(0, 3)], axis=0).T.astype(bf16)

    def block(i, slot, values):
        acc = jnp.zeros((nrhs, leaf), f32)
        for t in range(leaf // tile):
            power = nn(source[slot, t * tile : (t + 1) * tile, :], target[i])
            kern = jnp.exp2(power * scale).astype(bf16)
            acc += nn(values(t), kern)
        return acc

    def own(j):
        return lambda t: joint_ref[dim:, j * leaf + t * tile : j * leaf + (t + 1) * tile]

    def edge(side):
        return lambda t: halo_ref[side, dim:, t * tile : (t + 1) * tile]

    def flagged(i, column, slot, values):
        flag = jnp.where(near_ref[i, column] >= 0, 1.0, 0.0).astype(f32)
        image_ref[:, i * leaf : (i + 1) * leaf] += flag * block(i, slot, values)

    def itself(i):
        wide, extra = parts(joint_ref[:dim, i * leaf : (i + 1) * leaf])
        put_source(i + 1, wide, extra)
        target[i] = jnp.concatenate([wide, extra(3, 0)], axis=0).astype(bf16)
        image_ref[:, i * leaf : (i + 1) * leaf] = block(i, i + 1, own(i))

    def beside(i):
        here = jnp.where(near_ref[i, 2] >= 0, 1.0, 0.0).astype(f32)
        there = jnp.where(near_ref[i + 1, 1] >= 0, 1.0, 0.0).astype(f32)
        mine = joint_ref[dim:, i * leaf : (i + 1) * leaf]
        values = own(i + 1)
        acc = jnp.zeros((nrhs, leaf), f32)
        for t in range(leaf // tile):
            power = nn(source[i + 2, t * tile : (t + 1) * tile, :], target[i])
            kern = jnp.exp2(power * scale).astype(bf16)
            acc += nn(values(t), kern)
            cols = slice((i + 1) * leaf + t * tile, (i + 1) * leaf + (t + 1) * tile)
            image_ref[:, cols] += there * nt(mine, kern)
        image_ref[:, i * leaf : (i + 1) * leaf] += here * acc

    jobs = [functools.partial(itself, i) for i in range(leaf_dev)]
    jobs += [functools.partial(beside, i) for i in range(leaf_dev - 1)]

    pl.semaphore_wait(barrier, len(greeted))

    last = joint_ref.shape[1] - leaf
    halos = [
        pltpu.make_async_remote_copy(
            src_ref=joint_ref.at[:, pl.ds(last, leaf)], dst_ref=halo_ref.at[0],
            send_sem=halo_send.at[0], recv_sem=halo_recv.at[0], device_id=right_id, device_id_type=MESH,
        ),
        pltpu.make_async_remote_copy(
            src_ref=joint_ref.at[:, pl.ds(0, leaf)], dst_ref=halo_ref.at[1],
            send_sem=halo_send.at[1], recv_sem=halo_recv.at[1], device_id=left_id, device_id_type=MESH,
        ),
    ]

    def coupled(n):
        bit, _, _, b_ref, k = levels[n]
        other = got[n]
        mat = b_ref[k]
        return fold(jnp.where(bit == 0, nt(other, mat), nn(other, mat)))

    records = []
    for n, (bit, partner, q_ref, b_ref, k) in enumerate(levels):
        holder = sent.at[n]
        copy = pltpu.make_async_remote_copy(
            src_ref=holder, dst_ref=got.at[n], send_sem=node_send.at[n], recv_sem=node_recv.at[n],
            device_id=partner, device_id_type=MESH,
        )
        copy.start()
        if n == inner:
            for halo in halos:
                halo.start()
        if n > 0:
            records.append(coupled(n - 1))
        final = n == len(levels) - 1
        if not final:
            mine = nn(holder[...], q_ref[k, bit])
        for job in jobs[n * len(jobs) // len(levels) : (n + 1) * len(jobs) // len(levels)]:
            job()
        copy.wait()
        if not final:
            sent[n + 1] = split(fold(mine + nn(got[n], q_ref[k, 1 - bit])))
    incoming = coupled(len(levels) - 1)
    for n in reversed(range(len(levels) - 1)):
        bit, _, q_ref, _, k = levels[n]
        incoming = records[n] + fold(nt(split(incoming), q_ref[k, bit]))

    stacked = split(incoming)
    loads[matrices - 1].wait()
    for i in range(leaf_dev):
        cols = slice(i * leaf, (i + 1) * leaf)
        leaf_in = fold(nt(stacked, trans_ref[i])).astype(bf16)
        image_ref[:, cols] += ridge * direction_ref[:, cols] + nt(leaf_in, bases_ref[i])

    for side, (i, column, slot) in enumerate([(0, 1, 0), (leaf_dev - 1, 2, leaf_dev + 1)]):
        halos[side].wait()
        put_source(slot, *parts(halo_ref[side, :dim, :]))
        flagged(i, column, slot, edge(side))

    sums = [jnp.zeros((nrhs, 128), f32)] * 4

    def narrow(value):
        out = value[:, :128]
        for c in range(1, value.shape[1] // 128):
            out += value[:, c * 128 : (c + 1) * 128]
        return out

    for i in range(leaf_dev):
        cols = slice(i * leaf, (i + 1) * leaf)
        way = direction_ref[:, cols]
        rest = residual_ref[:, cols]
        image = image_ref[:, cols]
        terms = (rest * rest, way * image, rest * image, image * image)
        sums = [s + narrow(t) for s, t in zip(sums, terms)]
    rows = [jnp.sum(s.T, axis=0, keepdims=True) for s in sums]
    first[pos] = jnp.concatenate(rows + [jnp.zeros((4, nrhs), f32)], axis=0)

    def exchange(slots, mine, count, send, recv, where):
        def copy(o, slot):
            return pltpu.make_async_remote_copy(
                src_ref=slots.at[slot], dst_ref=slots.at[slot], send_sem=send.at[o], recv_sem=recv.at[slot],
                device_id=where(lax.rem(mine + o, count)), device_id_type=MESH,
            )

        for o in range(1, count):
            copy(o, mine).start()
        for o in range(1, count):
            copy(o, lax.rem(mine + o, count)).wait_recv()
        for o in range(1, count):
            copy(o, mine).wait_send()
        out = slots[0]
        for s in range(1, count):
            out += slots[s]
        return out

    second[grp] = exchange(first, pos, leaves, first_send, first_recv, lambda t: (grp, t))
    sums_ref[...] = exchange(second, grp, groups, second_send, second_recv, lambda t: (t, pos))


def update_kernel(sums_ref, x_ref, r_ref, d_ref, image_ref, new_x, new_r, new_d):
    rr, pq, rq, qq = [sums_ref[c : c + 1, :] for c in range(4)]
    alpha = rr / pq
    fresh = rr - 2.0 * alpha * rq + alpha * alpha * qq
    nrhs = x_ref.shape[0]
    square = (nrhs, nrhs)
    diagonal = lax.broadcasted_iota(jnp.int32, square, 0) == lax.broadcasted_iota(jnp.int32, square, 1)

    def column(row):
        return jnp.sum(jnp.where(diagonal, jnp.broadcast_to(row, square), 0.0), axis=1, keepdims=True)

    step, blend = column(alpha), column(fresh / rr)
    way = d_ref[...]
    new_x[...] = x_ref[...] + step * way
    rest = r_ref[...] - step * image_ref[...]
    new_r[...] = rest
    new_d[...] = rest + blend * way


def body(groups, leaves, points, solution, residual, direction, near, bases, leaf_transfer,
         inner_transfer, inner_coupling, outer_transfer, outer_coupling):
    leaf_dev = near.shape[0]
    leaf, rank = bases.shape[1:]
    count, dim = points.shape
    nrhs = direction.shape[1]
    rows = dim + nrhs
    levels = inner_transfer.shape[0] + outer_transfer.shape[0]
    p, x, r, d = points.T, solution.T, residual.T, direction.T
    anywhere = pl.BlockSpec(memory_space=pl.ANY)
    sems = pltpu.SemaphoreType.DMA
    image, sums = pl.pallas_call(
        functools.partial(step_kernel, groups, leaves),
        in_specs=[smem] + [anywhere] * 9,
        out_specs=[vmem] * 2,
        out_shape=[
            jax.ShapeDtypeStruct((nrhs, count), f32),
            jax.ShapeDtypeStruct((8, nrhs), f32),
        ],
        scratch_shapes=[
            pltpu.VMEM(inner_transfer.shape, bf16),
            pltpu.VMEM(inner_coupling.shape, bf16),
            pltpu.VMEM(outer_transfer.shape, bf16),
            pltpu.VMEM(outer_coupling.shape, bf16),
            pltpu.VMEM((rows, count), bf16),
            pltpu.VMEM((levels, 2 * nrhs, rank), bf16),
            pltpu.VMEM((levels, 2 * nrhs, rank), bf16),
            pltpu.VMEM((2, rows, leaf), bf16),
            pltpu.VMEM((leaf_dev + 2, leaf, 128), bf16),
            pltpu.VMEM((leaf_dev, 128, leaf), bf16),
            pltpu.VMEM(leaf_transfer.shape, bf16),
            pltpu.VMEM(bases.shape, bf16),
            pltpu.VMEM((nrhs, count), f32),
            pltpu.VMEM((nrhs, count), f32),
            pltpu.VMEM((leaves, 8, nrhs), f32),
            pltpu.VMEM((groups, 8, nrhs), f32),
            sems((levels,)), sems((levels,)), sems((2,)), sems((2,)),
            sems((leaves,)), sems((leaves,)), sems((groups,)), sems((groups,)), sems((leaf_dev + 8,)),
        ],
        compiler_params=pltpu.CompilerParams(collective_id=0, has_side_effects=True),
        name="step",
    )(near, inner_transfer, inner_coupling, outer_transfer, outer_coupling, p, leaf_transfer, bases, d, r)
    wide = pl.BlockSpec((nrhs, leaf), lambda i: (0, i))
    outs = pl.pallas_call(
        update_kernel,
        grid=(leaf_dev,),
        in_specs=[pl.BlockSpec((8, nrhs), lambda i: (0, 0))] + [wide] * 4,
        out_specs=[wide] * 3,
        out_shape=[jax.ShapeDtypeStruct((nrhs, count), f32)] * 3,
        name="update",
    )(sums, x, r, d, image)
    return tuple(out.T for out in outs)


def solution(mesh):
    both = ("grp", "leaf")
    flat = P(both, None)
    deep = P(both, None, None)
    return jax.shard_map(
        functools.partial(body, mesh.shape["grp"], mesh.shape["leaf"]),
        mesh=mesh,
        in_specs=(flat, flat, flat, flat, flat, deep, deep, P(), P(), P(), P()),
        out_specs=(flat, flat, flat),
        check_vma=False,
    )
```
